32 devices in a mesh: row: 16 (over z, x, core), col: 1, chan: 2 (over y).
Axes of the slice: x: 2, y: 2, z: 4, core: 2. Of those that a mesh axis runs over, the one named last changes fastest.
Arguments:
- array_volts: bfloat16 [6, 2, 128, 2048], P('chan', None, ('row', 'col')), parts along dimension 0, may hold values from -15 to 15, as said below
- reference_volts: bfloat16 [6, 2, 32, 2048], P('chan', None, None, 'col'), parts along dimension 0, may hold values from -15 to 15, as said below
Outputs:
- cleaned: float32 [6, 2, 128, 128], P('chan', None, 'row', 'col'), parts along dimension 0
The draws below stay inside these ranges and needn't reach their ends.
There are 2 independent parts, one for each index of `chan`. The reference program is written for one: setup_inputs(seed, part) draws one part's arguments, and reference() takes and returns one part's arrays. A program takes and returns all parts, laid end to end along the dimension named above; each array names one. Nothing has to cross between parts.
Inputs may be any that keep to these rules, and one draw needn't show every extreme that they name: `array_volts`: array voltages: common interference from a few sources plus independent noise. `reference_volts`: reference voltages: the same interference sources seen with other gains, plus independent noise.
All inputs are finite; a program needn't handle non-finite values.
Results may differ from the reference program's by a relative error of at most 0.0003.
Values may be sent and summed in bfloat16 or wider, within the bound.
No kernel may reach another device: no remote copies, remote signals or barrier semaphores. Data moves between devices by JAX's collectives and lax.ppermute only.
A program may use at most 64 MiB of HBM per device.

```python
import jax
import jax.numpy as jnp
from jax import lax

DEVICE_ANTENNAS = 8
NREF = 32
SUBINT_SAMPLES = 2048
SUBS = 3
NA = 128
N_ROW = 16
N_COL = 1


rfi_sources = 16


def common_signal(key):
    signal_key = jax.random.fold_in(key, 7001)
    return jax.random.normal(signal_key, (SUBS, 2, rfi_sources, SUBINT_SAMPLES), jnp.float32) * 0.7071


def apply_gains(gains, signal):
    real_part = jnp.einsum('nk,skt->snt', gains[0], signal[:, 0]) - jnp.einsum('nk,skt->snt', gains[1], signal[:, 1])
    imaginary_portion = jnp.einsum('nk,skt->snt', gains[0], signal[:, 1]) + jnp.einsum('nk,skt->snt', gains[1], signal[:, 0])
    return jnp.stack([real_part, imaginary_portion], 1)


def noise_field(key, count):
    scale_key = jax.random.fold_in(key, 1)
    value_key = jax.random.fold_in(key, 2)
    scales = jnp.exp(jax.random.uniform(scale_key, (count, 1), jnp.float32, jnp.log(0.5), jnp.log(1.5)))
    values = jax.random.normal(value_key, (SUBS, 2, count, SUBINT_SAMPLES), jnp.float32)
    return values * 0.7071 * scales


def draw_array_volts(key, part):
    signal = common_signal(key)
    gains = jax.random.normal(jax.random.fold_in(key, 7002), (2, NA, rfi_sources), jnp.float32) * jnp.sqrt(2.0 / rfi_sources)
    noise = noise_field(jax.random.fold_in(key, 7003), NA)
    return jnp.clip(apply_gains(gains, signal) + noise, -15.0, 15.0).astype(jnp.bfloat16)


def draw_reference_volts(key, part):
    signal = common_signal(key)
    gains = jax.random.normal(jax.random.fold_in(key, 7004), (2, NREF, rfi_sources), jnp.float32) * jnp.sqrt(0.05)
    noise = noise_field(jax.random.fold_in(key, 7005), NREF)
    return jnp.clip(apply_gains(gains, signal) + noise, -15.0, 15.0).astype(jnp.bfloat16)


def setup_inputs(seed: int = 0, part: int = 0) -> dict:
    key_list = jax.random.split(jax.random.key(seed), 3)
    part_keys = jax.random.split(jax.random.fold_in(key_list[2], part), 3)
    return {
        "array_volts": draw_array_volts(jax.random.fold_in(jax.random.fold_in(key_list[2], part), 71), part),
        "reference_volts": draw_reference_volts(jax.random.fold_in(jax.random.fold_in(key_list[2], part), 71), part),
    }


def correlate(first_rows, second_rows):
    width_first = first_rows.shape[1]
    width_second = second_rows.shape[1]
    samples = first_rows.shape[2]
    stacked_first = first_rows.reshape(2 * width_first, samples).astype(jnp.float32)
    stacked_second = second_rows.reshape(2 * width_second, samples).astype(jnp.float32)
    product = jnp.einsum('xn,yn->xy', stacked_first, stacked_second, precision=lax.Precision.HIGHEST)
    real_part = product[:width_first, :width_second] + product[width_first:, width_second:]
    imaginary_portion = product[width_first:, :width_second] - product[:width_first, width_second:]
    return jnp.stack([real_part, imaginary_portion]) / jnp.float32(samples)

def subtract(vis_tile, rows_cross, cross_cols, reference_covariance):
    real_cov = reference_covariance[0]
    imag_cov = reference_covariance[1]
    system = jnp.concatenate([jnp.concatenate([real_cov, -imag_cov], 1), jnp.concatenate([imag_cov, real_cov], 1)], 0)
    lower_factor = jnp.linalg.cholesky(system)
    right_hand = jnp.concatenate([cross_cols[0], cross_cols[1]], 0)
    middle = lax.linalg.triangular_solve(lower_factor, right_hand, left_side=True, lower=True)
    solved = lax.linalg.triangular_solve(lower_factor, middle, left_side=True, lower=True, transpose_a=True)
    half_size = real_cov.shape[0]
    solved_real = solved[:half_size]
    solved_imag = solved[half_size:]
    highest = lax.Precision.HIGHEST
    corr_real = jnp.dot(rows_cross[0], solved_real, precision=highest) - jnp.dot(rows_cross[1], solved_imag, precision=highest)
    corr_imag = jnp.dot(rows_cross[0], solved_imag, precision=highest) + jnp.dot(rows_cross[1], solved_real, precision=highest)
    return vis_tile - jnp.stack([corr_real, corr_imag])

def reference(array_volts, reference_volts):
    results = []
    for sub_index in range(SUBS):
        complete_matrix = array_volts[sub_index]
        antenna_list = complete_matrix.shape[1]
        permuted_rows = complete_matrix.reshape(2, N_ROW, N_COL, DEVICE_ANTENNAS, SUBINT_SAMPLES).transpose(0, 2, 1, 3, 4).reshape(2, antenna_list, SUBINT_SAMPLES)
        ref_all = reference_volts[sub_index]
        vis_tile = correlate(complete_matrix, permuted_rows)
        rows_cross = correlate(complete_matrix, ref_all)
        cross_cols = correlate(ref_all, permuted_rows)
        reference_covariance = correlate(ref_all, ref_all)
        results.append(subtract(vis_tile, rows_cross, cross_cols, reference_covariance))
    return jnp.stack(results)
```

```python
import functools

import jax
import jax.numpy as jnp
from jax import lax
from jax.experimental import pallas as pl
from jax.experimental.pallas import tpu as pltpu
from jax.sharding import PartitionSpec as P

LANES = 128
NT = (((1,), (1,)), ((), ()))
TN = (((0,), (0,)), ((), ()))
TT = (((0,), (1,)), ((), ()))
HIGHEST = lax.Precision.HIGHEST


def correlate(first_rows, second_rows):
    width_first = first_rows.shape[1]
    width_second = second_rows.shape[1]
    samples = first_rows.shape[2]
    stacked_first = first_rows.reshape(2 * width_first, samples)
    stacked_second = second_rows.reshape(2 * width_second, samples)
    product = jnp.einsum(
        "xn,yn->xy", stacked_first, stacked_second, preferred_element_type=jnp.float32
    )
    real_part = product[:width_first, :width_second] + product[width_first:, width_second:]
    imaginary_portion = product[width_first:, :width_second] - product[:width_first, width_second:]
    return jnp.stack([real_part, imaginary_portion]) / jnp.float32(samples)


def conj_swap(cross_block):
    return jnp.stack([cross_block[0].T, -cross_block[1].T])


def subtract(vis_tile, rows_cross, cross_cols, reference_covariance):
    real_cov = reference_covariance[0]
    imag_cov = reference_covariance[1]
    system = jnp.concatenate(
        [jnp.concatenate([real_cov, -imag_cov], 1), jnp.concatenate([imag_cov, real_cov], 1)], 0
    )
    lower_factor = jnp.linalg.cholesky(system)
    right_hand = jnp.concatenate([cross_cols[0], cross_cols[1]], 0)
    middle = lax.linalg.triangular_solve(lower_factor, right_hand, left_side=True, lower=True)
    solved = lax.linalg.triangular_solve(
        lower_factor, middle, left_side=True, lower=True, transpose_a=True
    )
    half_size = real_cov.shape[0]
    solved_real = solved[:half_size]
    solved_imag = solved[half_size:]
    corr_real = jnp.dot(rows_cross[0], solved_real, precision=HIGHEST) - jnp.dot(
        rows_cross[1], solved_imag, precision=HIGHEST
    )
    corr_imag = jnp.dot(rows_cross[0], solved_imag, precision=HIGHEST) + jnp.dot(
        rows_cross[1], solved_real, precision=HIGHEST
    )
    return vis_tile - jnp.stack([corr_real, corr_imag])


def per_device_any(array_volts, reference_volts):
    results = []
    for sub_index in range(array_volts.shape[0]):
        local_volts = array_volts[sub_index]
        ref_all = lax.all_gather(reference_volts[sub_index], "col", axis=2, tiled=True)
        reference_covariance = correlate(ref_all, ref_all)
        own_cross = correlate(ref_all, local_volts)
        cross_row_block = lax.all_gather(own_cross, "col", axis=2, tiled=True)
        cross_cols = lax.all_gather(own_cross, "row", axis=2, tiled=True)
        rows_cross = conj_swap(cross_row_block)
        row_volts = lax.all_gather(local_volts, "col", axis=1, tiled=True)
        joined = correlate(row_volts, lax.all_gather(local_volts, "row", axis=1, tiled=True))
        results.append(subtract(joined, rows_cross, cross_cols, reference_covariance))
    return jnp.stack(results)


def pack_body(volts_ref, reference_ref, message_ref, *, group):
    subs, _, ants, samples = volts_ref.shape
    members = message_ref.shape[0]
    share = samples // group
    tiles = share // LANES
    base = subs * 2 * tiles * ants
    for s in range(subs):
        real, imag = volts_ref[s, 0], volts_ref[s, 1]
        ref_real, ref_imag = reference_ref[s, 0], reference_ref[s, 1]
        cross = lax.dot_general(
            real, jnp.concatenate([ref_real, -ref_imag], 0), NT, preferred_element_type=jnp.float32
        ) + lax.dot_general(
            imag, jnp.concatenate([ref_imag, ref_real], 0), NT, preferred_element_type=jnp.float32
        )
        cross = cross / jnp.float32(samples)
        high = cross.astype(jnp.bfloat16)
        low = (cross - high.astype(jnp.float32)).astype(jnp.bfloat16)
        both = jnp.concatenate([high, low], 1)
        for m in range(members):
            message_ref[m, base + s * ants : base + (s + 1) * ants, :] = both
            for p in range(2):
                for t in range(tiles):
                    at = ((s * 2 + p) * tiles + t) * ants
                    start = (m % group) * share + t * LANES
                    message_ref[m, at : at + ants, :] = volts_ref[s, p, :, start : start + LANES]


def solve_body(volts_ref, reference_ref, solved_ref):
    subs, _, ants, samples = volts_ref.shape
    nref = reference_ref.shape[2]
    reals, imags = [], []
    for s in range(subs):
        real, imag = volts_ref[s, 0], volts_ref[s, 1]
        ref_real, ref_imag = reference_ref[s, 0], reference_ref[s, 1]
        first = jnp.concatenate([ref_real, real], 0)
        second = jnp.concatenate([ref_imag, imag], 0)
        dot = functools.partial(
            lax.dot_general, dimension_numbers=NT, preferred_element_type=jnp.float32
        )
        reals.append((dot(ref_real, first) + dot(ref_imag, second)) / jnp.float32(samples))
        imags.append((dot(ref_imag, first) - dot(ref_real, second)) / jnp.float32(samples))
    re, im = jnp.stack(reals), jnp.stack(imags)
    rows = lax.broadcasted_iota(jnp.int32, (1, nref, 1), 1)
    for i in range(nref):
        inverse = 1.0 / re[:, i : i + 1, i : i + 1]
        row_re, row_im = re[:, i : i + 1, :] * inverse, im[:, i : i + 1, :] * inverse
        col_re, col_im = re[:, :, i : i + 1], im[:, :, i : i + 1]
        here = rows == i
        re, im = (
            jnp.where(here, row_re, re - (col_re * row_re - col_im * row_im)),
            jnp.where(here, row_im, im - (col_re * row_im + col_im * row_re)),
        )
    solved_ref[:, 0] = re[:, :, nref:]
    solved_ref[:, 1] = im[:, :, nref:]


def joined(block):
    members, ants, lanes = block.shape
    return block.astype(jnp.float32).reshape(members * ants, lanes)


def product_body(message_ref, partial_ref, *, group, subs, ants):
    members = message_ref.shape[0]
    rows = partial_ref.shape[1] // (subs * 2)
    tiles = (message_ref.shape[1] // ants - subs) // (subs * 2)
    mine = (lax.axis_index("row") // group) * group
    for s in range(subs):
        cols, own = [], []
        for p in range(2):
            for t in range(tiles):
                at = ((s * 2 + p) * tiles + t) * ants
                cols.append(joined(message_ref[:, at : at + ants, :]).astype(jnp.bfloat16))
                own.append(joined(message_ref[pl.ds(mine, group), at : at + ants, :]))
        right = jnp.concatenate(cols, 1)
        upper = jnp.concatenate(own, 1)
        lower = jnp.concatenate(own[tiles:] + [-x for x in own[:tiles]], 1)
        left = jnp.concatenate([upper, lower], 0).astype(jnp.bfloat16)
        out = lax.dot_general(left, right, NT, preferred_element_type=jnp.float32)
        height = group * ants
        for p in range(2):
            at = (s * 2 + p) * rows
            partial_ref[:, at : at + rows, :] = out[p * height : (p + 1) * height].reshape(
                group, ants, members * ants
            )


def correction_body(message_ref, solved_ref, correction_ref):
    subs, _, nref, ants = solved_ref.shape
    base = message_ref.shape[1] - subs * ants
    for s in range(subs):
        cross = joined(message_ref[:, base + s * ants : base + (s + 1) * ants, :])
        re, im = solved_ref[s, 0], solved_ref[s, 1]
        for p, stack in enumerate(([re, -im], [-im, -re])):
            column = jnp.concatenate(stack + stack, 0)
            correction_ref[s, p] = lax.dot_general(
                column, cross, TT, precision=HIGHEST, preferred_element_type=jnp.float32
            )


def finish_body(partial_ref, correction_ref, cleaned_ref, *, samples):
    subs, _, ants, _ = cleaned_ref.shape
    total = partial_ref[0]
    for m in range(1, partial_ref.shape[0]):
        total = total + partial_ref[m]
    total = total / jnp.float32(samples)
    for s in range(subs):
        for p in range(2):
            at = (s * 2 + p) * ants
            cleaned_ref[s, p] = total[at : at + ants] - correction_ref[s, p]


def call(body, out, *args, flops=0, moved=0, **kw):
    spec = pl.BlockSpec(memory_space=pltpu.VMEM)
    return pl.pallas_call(
        functools.partial(body, **kw) if kw else body,
        out_shape=out,
        in_specs=[spec] * len(args),
        out_specs=spec,
        cost_estimate=pl.CostEstimate(flops=flops, bytes_accessed=moved, transcendentals=0),
        name=body.__name__,
    )(*args)


def per_device(array_volts, reference_volts, *, n_row):
    subs, _, ants, samples = array_volts.shape
    nref = reference_volts.shape[2]
    group = n_row // 2
    tiles = samples // group // LANES
    f32 = functools.partial(jax.ShapeDtypeStruct, dtype=jnp.float32)
    height = subs * 2 * tiles * ants + subs * ants
    message = call(
        pack_body,
        jax.ShapeDtypeStruct((n_row, height, LANES), jnp.bfloat16),
        array_volts,
        reference_volts,
        group=group,
    )
    volts = lax.all_to_all(message, "row", split_axis=0, concat_axis=0, tiled=True)
    solved = call(
        solve_body,
        f32((subs, 2, nref, ants)),
        array_volts,
        reference_volts,
        flops=10**9,
        moved=2 * 10**7,
    )
    partial = call(
        product_body,
        f32((group, subs * 2 * ants, n_row * ants)),
        volts,
        group=group,
        subs=subs,
        ants=ants,
    )
    groups = [list(range(group)), list(range(group, n_row))]
    sums = lax.all_to_all(
        partial, "row", split_axis=0, concat_axis=0, tiled=True, axis_index_groups=groups
    )
    correction = call(
        correction_body,
        f32((subs, 2, ants, n_row * ants)),
        volts,
        solved,
        flops=10**8,
        moved=2 * 10**6,
    )
    return call(
        finish_body, f32((subs, 2, ants, n_row * ants)), sums, correction, samples=samples
    )


def solution(mesh):
    n_row, n_col = mesh.shape["row"], mesh.shape["col"]

    def body(array_volts, reference_volts):
        samples = array_volts.shape[3]
        nref = reference_volts.shape[2]
        split = n_col == 1 and n_row % 2 == 0 and samples % (n_row // 2 * LANES) == 0
        if split and 4 * nref == LANES:
            return per_device(array_volts, reference_volts, n_row=n_row)
        return per_device_any(array_volts, reference_volts)

    return jax.shard_map(
        body,
        mesh=mesh,
        in_specs=(P("chan", None, ("row", "col"), None), P("chan", None, None, "col")),
        out_specs=P("chan", None, "row", "col"),
        check_vma=False,
    )
```

```python
import functools

import jax
import jax.numpy as jnp
from jax import lax
from jax.experimental import pallas as pl
from jax.experimental.pallas import tpu as pltpu
from jax.sharding import PartitionSpec as P

LANES = 128
GRANT = 16 * 1024 * 1024
NT = (((1,), (1,)), ((), ()))
TN = (((0,), (0,)), ((), ()))
TT = (((0,), (1,)), ((), ()))
HIGHEST = lax.Precision.HIGHEST


def correlate(first_rows, second_rows):
    width_first = first_rows.shape[1]
    width_second = second_rows.shape[1]
    samples = first_rows.shape[2]
    stacked_first = first_rows.reshape(2 * width_first, samples)
    stacked_second = second_rows.reshape(2 * width_second, samples)
    product = jnp.einsum(
        "xn,yn->xy", stacked_first, stacked_second, preferred_element_type=jnp.float32
    )
    real_part = product[:width_first, :width_second] + product[width_first:, width_second:]
    imaginary_portion = product[width_first:, :width_second] - product[:width_first, width_second:]
    return jnp.stack([real_part, imaginary_portion]) / jnp.float32(samples)


def conj_swap(cross_block):
    return jnp.stack([cross_block[0].T, -cross_block[1].T])


def subtract(vis_tile, rows_cross, cross_cols, reference_covariance):
    real_cov = reference_covariance[0]
    imag_cov = reference_covariance[1]
    system = jnp.concatenate(
        [jnp.concatenate([real_cov, -imag_cov], 1), jnp.concatenate([imag_cov, real_cov], 1)], 0
    )
    lower_factor = jnp.linalg.cholesky(system)
    right_hand = jnp.concatenate([cross_cols[0], cross_cols[1]], 0)
    middle = lax.linalg.triangular_solve(lower_factor, right_hand, left_side=True, lower=True)
    solved = lax.linalg.triangular_solve(
        lower_factor, middle, left_side=True, lower=True, transpose_a=True
    )
    half_size = real_cov.shape[0]
    solved_real = solved[:half_size]
    solved_imag = solved[half_size:]
    corr_real = jnp.dot(rows_cross[0], solved_real, precision=HIGHEST) - jnp.dot(
        rows_cross[1], solved_imag, precision=HIGHEST
    )
    corr_imag = jnp.dot(rows_cross[0], solved_imag, precision=HIGHEST) + jnp.dot(
        rows_cross[1], solved_real, precision=HIGHEST
    )
    return vis_tile - jnp.stack([corr_real, corr_imag])


def per_device_any(array_volts, reference_volts):
    results = []
    for sub_index in range(array_volts.shape[0]):
        local_volts = array_volts[sub_index]
        ref_all = lax.all_gather(reference_volts[sub_index], "col", axis=2, tiled=True)
        reference_covariance = correlate(ref_all, ref_all)
        own_cross = correlate(ref_all, local_volts)
        cross_row_block = lax.all_gather(own_cross, "col", axis=2, tiled=True)
        cross_cols = lax.all_gather(own_cross, "row", axis=2, tiled=True)
        rows_cross = conj_swap(cross_row_block)
        row_volts = lax.all_gather(local_volts, "col", axis=1, tiled=True)
        joined = correlate(row_volts, lax.all_gather(local_volts, "row", axis=1, tiled=True))
        results.append(subtract(joined, rows_cross, cross_cols, reference_covariance))
    return jnp.stack(results)


def pack_body(volts_ref, message_ref, *, group):
    subs, _, ants, samples = volts_ref.shape
    members = message_ref.shape[0]
    share = samples // group
    tiles = share // LANES
    for s in range(subs):
        for p in range(2):
            for c in range(group):
                for t in range(tiles):
                    at = ((s * 2 + p) * tiles + t) * ants
                    start = c * share + t * LANES
                    block = volts_ref[s, p, :, start : start + LANES]
                    for m in range(c, members, group):
                        message_ref[m, at : at + ants, :] = block


def cross_body(volts_ref, reference_ref, message_ref):
    subs, _, ants, samples = volts_ref.shape
    crosses = []
    for s in range(subs):
        real, imag = volts_ref[s, 0], volts_ref[s, 1]
        ref_real, ref_imag = reference_ref[s, 0], reference_ref[s, 1]
        cross = lax.dot_general(
            real, jnp.concatenate([ref_real, -ref_imag], 0), NT, preferred_element_type=jnp.float32
        ) + lax.dot_general(
            imag, jnp.concatenate([ref_imag, ref_real], 0), NT, preferred_element_type=jnp.float32
        )
        crosses.append(cross / jnp.float32(samples))
    if subs % 2:
        crosses.append(jnp.zeros_like(crosses[0]))
    for pair in range(len(crosses) // 2):
        message_ref[0, pair * ants : (pair + 1) * ants, :] = jnp.concatenate(
            crosses[2 * pair : 2 * pair + 2], 1
        )


def solve_body(volts_ref, reference_ref, solved_ref):
    subs, _, ants, samples = volts_ref.shape
    nref = reference_ref.shape[2]
    reals, imags = [], []
    for s in range(subs):
        real, imag = volts_ref[s, 0], volts_ref[s, 1]
        ref_real, ref_imag = reference_ref[s, 0], reference_ref[s, 1]
        first = jnp.concatenate([ref_real, real], 0)
        second = jnp.concatenate([ref_imag, imag], 0)
        dot = functools.partial(
            lax.dot_general, dimension_numbers=NT, preferred_element_type=jnp.float32
        )
        reals.append((dot(ref_real, first) + dot(ref_imag, second)) / jnp.float32(samples))
        imags.append((dot(ref_imag, first) - dot(ref_real, second)) / jnp.float32(samples))
    re, im = jnp.stack(reals), jnp.stack(imags)
    rows = lax.broadcasted_iota(jnp.int32, (1, nref, 1), 1)
    for i in range(nref):
        inverse = 1.0 / re[:, i : i + 1, i : i + 1]
        row_re, row_im = re[:, i : i + 1, :] * inverse, im[:, i : i + 1, :] * inverse
        col_re, col_im = re[:, :, i : i + 1], im[:, :, i : i + 1]
        here = rows == i
        re, im = (
            jnp.where(here, row_re, re - (col_re * row_re - col_im * row_im)),
            jnp.where(here, row_im, im - (col_re * row_im + col_im * row_re)),
        )
    solved_ref[:, 0] = re[:, :, nref:]
    solved_ref[:, 1] = im[:, :, nref:]


def joined(block):
    members, ants, lanes = block.shape
    return block.astype(jnp.float32).reshape(members * ants, lanes)


def product_body(message_ref, partial_ref, *, group, subs, ants):
    members = message_ref.shape[0]
    rows = partial_ref.shape[1] // (subs * 2)
    tiles = message_ref.shape[1] // (ants * subs * 2)
    mine = (lax.axis_index("row") // group) * group
    for s in range(subs):
        cols, own = [], []
        for p in range(2):
            for t in range(tiles):
                at = ((s * 2 + p) * tiles + t) * ants
                cols.append(joined(message_ref[:, at : at + ants, :]).astype(jnp.bfloat16))
                own.append(joined(message_ref[pl.ds(mine, group), at : at + ants, :]))
        right = jnp.concatenate(cols, 1)
        upper = jnp.concatenate(own, 1)
        lower = jnp.concatenate(own[tiles:] + [-x for x in own[:tiles]], 1)
        left = jnp.concatenate([upper, lower], 0).astype(jnp.bfloat16)
        out = lax.dot_general(left, right, NT, preferred_element_type=jnp.float32)
        height = group * ants
        for p in range(2):
            at = (s * 2 + p) * rows
            partial_ref[:, at : at + rows, :] = out[p * height : (p + 1) * height].reshape(
                group, ants, members * ants
            )


def correction_body(cross_ref, solved_ref, correction_ref):
    subs, _, nref, ants = solved_ref.shape
    me = lax.axis_index("row")
    for pair in range((subs + 1) // 2):
        members = range(2 * pair, min(2 * pair + 2, subs))
        cross = jnp.concatenate(
            [
                cross_ref[jnp.bitwise_xor(me, j), pair * ants : (pair + 1) * ants, :]
                for j in range(cross_ref.shape[0])
            ],
            0,
        )
        columns = []
        for s in members:
            re, im = solved_ref[s, 0], solved_ref[s, 1]
            none = jnp.zeros((2 * nref, ants), jnp.float32)
            for stack in ([re, -im], [-im, -re]):
                columns.append(
                    jnp.concatenate(stack + [none] if s % 2 == 0 else [none] + stack, 0)
                )
        out = lax.dot_general(
            jnp.concatenate(columns, 1),
            cross,
            TT,
            precision=HIGHEST,
            preferred_element_type=jnp.float32,
        )
        for k, s in enumerate(members):
            for p in range(2):
                at = (2 * k + p) * ants
                correction_ref[s, p] = out[at : at + ants]


def finish_body(partial_ref, correction_ref, cleaned_ref, *, samples):
    subs, _, ants, _ = cleaned_ref.shape
    total = partial_ref[0]
    for m in range(1, partial_ref.shape[0]):
        total = total + partial_ref[m]
    total = total / jnp.float32(samples)
    for s in range(subs):
        for p in range(2):
            at = (s * 2 + p) * ants
            cleaned_ref[s, p] = total[at : at + ants] - correction_ref[s, p]


def call(body, out, *args, inner=(), flops=0, moved=0, **kw):
    spec = pl.BlockSpec(memory_space=pltpu.VMEM)
    args = [
        pltpu.with_memory_space_constraint(x, pltpu.VMEM) if i in inner else x
        for i, x in enumerate(args)
    ]
    return pl.pallas_call(
        functools.partial(body, **kw) if kw else body,
        out_shape=out,
        in_specs=[spec] * len(args),
        out_specs=spec,
        compiler_params=pltpu.CompilerParams(vmem_limit_bytes=GRANT),
        cost_estimate=pl.CostEstimate(flops=flops, bytes_accessed=moved, transcendentals=0),
        name=body.__name__,
    )(*args)


def per_device(array_volts, reference_volts, *, n_row):
    subs, _, ants, samples = array_volts.shape
    nref = reference_volts.shape[2]
    group = n_row // 2
    tiles = samples // group // LANES
    f32 = jnp.float32
    height = subs * 2 * tiles * ants
    message = call(
        pack_body,
        jax.ShapeDtypeStruct((n_row, height, LANES), jnp.bfloat16),
        array_volts,
        group=group,
    )
    volts = lax.all_to_all(message, "row", split_axis=0, concat_axis=0, tiled=True)
    crosses = call(
        cross_body,
        jax.ShapeDtypeStruct((1, (subs + 1) // 2 * ants, LANES), f32),
        array_volts,
        reference_volts,
        flops=10**8,
        moved=10**6,
    )
    bit = 1
    while bit < n_row:
        other = lax.ppermute(crosses, "row", [(i, i ^ bit) for i in range(n_row)])
        if 2 * bit == n_row:
            volts, crosses = lax.optimization_barrier((volts, crosses))
        crosses = jnp.concatenate([crosses, other], 0)
        bit *= 2
    solved = call(
        solve_body,
        pltpu.VMEM((subs, 2, nref, ants), f32),
        array_volts,
        reference_volts,
        flops=10**9,
        moved=2 * 10**7,
    )
    partial = call(
        product_body,
        pltpu.VMEM((group, subs * 2 * ants, n_row * ants), f32),
        volts,
        inner=(0,),
        group=group,
        subs=subs,
        ants=ants,
    )
    groups = [list(range(group)), list(range(group, n_row))]
    sums = lax.all_to_all(
        partial, "row", split_axis=0, concat_axis=0, tiled=True, axis_index_groups=groups
    )
    correction = call(
        correction_body,
        pltpu.VMEM((subs, 2, ants, n_row * ants), f32),
        crosses,
        solved,
        inner=(0, 1),
        flops=10**8,
        moved=2 * 10**6,
    )
    return call(
        finish_body,
        jax.ShapeDtypeStruct((subs, 2, ants, n_row * ants), f32),
        sums,
        correction,
        inner=(0, 1),
        samples=samples,
    )


def solution(mesh):
    n_row, n_col = mesh.shape["row"], mesh.shape["col"]

    def body(array_volts, reference_volts):
        samples = array_volts.shape[3]
        nref = reference_volts.shape[2]
        split = n_col == 1 and n_row > 1 and n_row & (n_row - 1) == 0 and samples % (n_row // 2 * LANES) == 0
        if split and 4 * nref == LANES:
            return per_device(array_volts, reference_volts, n_row=n_row)
        return per_device_any(array_volts, reference_volts)

    return jax.shard_map(
        body,
        mesh=mesh,
        in_specs=(P("chan", None, ("row", "col"), None), P("chan", None, None, "col")),
        out_specs=P("chan", None, "row", "col"),
        check_vma=False,
    )
```

```python
import functools

import jax
import jax.numpy as jnp
from jax import lax
from jax.experimental import pallas as pl
from jax.experimental.pallas import tpu as pltpu
from jax.sharding import PartitionSpec as P

LANES = 128
GRANT = 16 * 1024 * 1024
NT = (((1,), (1,)), ((), ()))
TN = (((0,), (0,)), ((), ()))
TT = (((0,), (1,)), ((), ()))
HIGHEST = lax.Precision.HIGHEST


def correlate(first_rows, second_rows):
    width_first = first_rows.shape[1]
    width_second = second_rows.shape[1]
    samples = first_rows.shape[2]
    stacked_first = first_rows.reshape(2 * width_first, samples)
    stacked_second = second_rows.reshape(2 * width_second, samples)
    product = jnp.einsum(
        "xn,yn->xy", stacked_first, stacked_second, preferred_element_type=jnp.float32
    )
    real_part = product[:width_first, :width_second] + product[width_first:, width_second:]
    imaginary_portion = product[width_first:, :width_second] - product[:width_first, width_second:]
    return jnp.stack([real_part, imaginary_portion]) / jnp.float32(samples)


def conj_swap(cross_block):
    return jnp.stack([cross_block[0].T, -cross_block[1].T])


def subtract(vis_tile, rows_cross, cross_cols, reference_covariance):
    real_cov = reference_covariance[0]
    imag_cov = reference_covariance[1]
    system = jnp.concatenate(
        [jnp.concatenate([real_cov, -imag_cov], 1), jnp.concatenate([imag_cov, real_cov], 1)], 0
    )
    lower_factor = jnp.linalg.cholesky(system)
    right_hand = jnp.concatenate([cross_cols[0], cross_cols[1]], 0)
    middle = lax.linalg.triangular_solve(lower_factor, right_hand, left_side=True, lower=True)
    solved = lax.linalg.triangular_solve(
        lower_factor, middle, left_side=True, lower=True, transpose_a=True
    )
    half_size = real_cov.shape[0]
    solved_real = solved[:half_size]
    solved_imag = solved[half_size:]
    corr_real = jnp.dot(rows_cross[0], solved_real, precision=HIGHEST) - jnp.dot(
        rows_cross[1], solved_imag, precision=HIGHEST
    )
    corr_imag = jnp.dot(rows_cross[0], solved_imag, precision=HIGHEST) + jnp.dot(
        rows_cross[1], solved_real, precision=HIGHEST
    )
    return vis_tile - jnp.stack([corr_real, corr_imag])


def per_device_any(array_volts, reference_volts):
    results = []
    for sub_index in range(array_volts.shape[0]):
        local_volts = array_volts[sub_index]
        ref_all = lax.all_gather(reference_volts[sub_index], "col", axis=2, tiled=True)
        reference_covariance = correlate(ref_all, ref_all)
        own_cross = correlate(ref_all, local_volts)
        cross_row_block = lax.all_gather(own_cross, "col", axis=2, tiled=True)
        cross_cols = lax.all_gather(own_cross, "row", axis=2, tiled=True)
        rows_cross = conj_swap(cross_row_block)
        row_volts = lax.all_gather(local_volts, "col", axis=1, tiled=True)
        joined = correlate(row_volts, lax.all_gather(local_volts, "row", axis=1, tiled=True))
        results.append(subtract(joined, rows_cross, cross_cols, reference_covariance))
    return jnp.stack(results)


def pack_body(volts_ref, message_ref, *, group):
    subs, _, ants, samples = volts_ref.shape
    members = message_ref.shape[0]
    share = samples // group
    tiles = share // LANES
    for s in range(subs):
        for p in range(2):
            for c in range(group):
                for t in range(tiles):
                    at = ((s * 2 + p) * tiles + t) * ants
                    start = c * share + t * LANES
                    block = volts_ref[s, p, :, start : start + LANES]
                    for m in range(c, members, group):
                        message_ref[m, at : at + ants, :] = block


def cross_body(volts_ref, reference_ref, message_ref):
    subs, _, ants, samples = volts_ref.shape
    crosses = []
    for s in range(subs):
        real, imag = volts_ref[s, 0], volts_ref[s, 1]
        ref_real, ref_imag = reference_ref[s, 0], reference_ref[s, 1]
        cross = lax.dot_general(
            real, jnp.concatenate([ref_real, -ref_imag], 0), NT, preferred_element_type=jnp.float32
        ) + lax.dot_general(
            imag, jnp.concatenate([ref_imag, ref_real], 0), NT, preferred_element_type=jnp.float32
        )
        crosses.append(cross / jnp.float32(samples))
    if subs % 2:
        crosses.append(jnp.zeros_like(crosses[0]))
    for pair in range(len(crosses) // 2):
        message_ref[0, pair * ants : (pair + 1) * ants, :] = jnp.concatenate(
            crosses[2 * pair : 2 * pair + 2], 1
        )


def system_body(volts_ref, reference_ref, system_ref):
    subs, _, ants, samples = volts_ref.shape
    nref = reference_ref.shape[2]
    dot = functools.partial(
        lax.dot_general, dimension_numbers=NT, preferred_element_type=jnp.float32
    )
    reals, imags = [], []
    for s in range(subs):
        real, imag = volts_ref[s, 0], volts_ref[s, 1]
        ref_real, ref_imag = reference_ref[s, 0], reference_ref[s, 1]
        first = jnp.concatenate([ref_real, real], 0)
        second = jnp.concatenate([ref_imag, imag], 0)
        reals.append((dot(ref_real, first) + dot(ref_imag, second)) / jnp.float32(samples))
        imags.append((dot(ref_imag, first) - dot(ref_real, second)) / jnp.float32(samples))
    re, im = eliminate(jnp.stack(reals), jnp.stack(imags), 0, nref // 2)
    system_ref[0], system_ref[1] = re, im


def solve_body(system_ref, solved_ref):
    nref = system_ref.shape[2]
    re, im = eliminate(system_ref[0], system_ref[1], nref // 2, nref)
    solved_ref[:, 0] = re[:, :, nref:]
    solved_ref[:, 1] = im[:, :, nref:]


def eliminate(re, im, start, stop):
    rows = lax.broadcasted_iota(jnp.int32, (1, re.shape[1], 1), 1)
    for i in range(start, stop):
        inverse = 1.0 / re[:, i : i + 1, i : i + 1]
        row_re, row_im = re[:, i : i + 1, :] * inverse, im[:, i : i + 1, :] * inverse
        col_re, col_im = re[:, :, i : i + 1], im[:, :, i : i + 1]
        here = rows == i
        re, im = (
            jnp.where(here, row_re, re - (col_re * row_re - col_im * row_im)),
            jnp.where(here, row_im, im - (col_re * row_im + col_im * row_re)),
        )
    return re, im


def joined(block):
    members, ants, lanes = block.shape
    return block.astype(jnp.float32).reshape(members * ants, lanes)


def product_body(message_ref, even_ref, odd_ref, *, group, subs, ants):
    members = message_ref.shape[0]
    tiles = message_ref.shape[1] // (ants * subs * 2)
    me = lax.axis_index("row")
    for s in range(subs):
        cols, own = [], []
        for p in range(2):
            for t in range(tiles):
                at = ((s * 2 + p) * tiles + t) * ants
                cols.append(joined(message_ref[:, at : at + ants, :]).astype(jnp.bfloat16))
                own.append(
                    jnp.concatenate(
                        [
                            message_ref[me ^ j, at : at + ants, :].astype(jnp.float32)
                            for j in range(group)
                        ],
                        0,
                    )
                )
        right = jnp.concatenate(cols, 1)
        upper = jnp.concatenate(own, 1)
        lower = jnp.concatenate(own[tiles:] + [-x for x in own[:tiles]], 1)
        left = jnp.concatenate([upper, lower], 0).astype(jnp.bfloat16)
        out = lax.dot_general(left, right, NT, preferred_element_type=jnp.float32)
        for p in range(2):
            at = (s * 2 + p) * ants
            for j in range(group):
                row = (p * group + j) * ants
                ref = odd_ref if j % 2 else even_ref
                ref[j // 2, at : at + ants, :] = out[row : row + ants]


def correction_body(cross_ref, solved_ref, correction_ref):
    subs, _, nref, ants = solved_ref.shape
    me = lax.axis_index("row")
    for pair in range((subs + 1) // 2):
        members = range(2 * pair, min(2 * pair + 2, subs))
        cross = jnp.concatenate(
            [
                cross_ref[me ^ m, pair * ants : (pair + 1) * ants, :]
                for m in range(cross_ref.shape[0])
            ],
            0,
        )
        columns = []
        for s in members:
            re, im = solved_ref[s, 0], solved_ref[s, 1]
            none = jnp.zeros((2 * nref, ants), jnp.float32)
            for stack in ([re, -im], [-im, -re]):
                columns.append(
                    jnp.concatenate(stack + [none] if s % 2 == 0 else [none] + stack, 0)
                )
        out = lax.dot_general(
            jnp.concatenate(columns, 1),
            cross,
            TT,
            precision=HIGHEST,
            preferred_element_type=jnp.float32,
        )
        for k, s in enumerate(members):
            for p in range(2):
                at = (2 * k + p) * ants
                correction_ref[s, p] = out[at : at + ants]


def finish_body(kept_ref, *refs, samples):
    *others, correction_ref, cleaned_ref = refs
    subs, _, ants, _ = cleaned_ref.shape
    total = kept_ref[0]
    for ref in others:
        total = total + ref[0]
    total = total / jnp.float32(samples)
    for s in range(subs):
        for p in range(2):
            at = (s * 2 + p) * ants
            cleaned_ref[s, p] = total[at : at + ants] - correction_ref[s, p]


def swap(x, bit, n_row):
    return lax.ppermute(x, "row", [(i, i ^ bit) for i in range(n_row)])


def call(body, out, *args, inner=(), flops=0, moved=0, **kw):
    spec = pl.BlockSpec(memory_space=pltpu.VMEM)
    args = [
        pltpu.with_memory_space_constraint(x, pltpu.VMEM) if i in inner else x
        for i, x in enumerate(args)
    ]
    return pl.pallas_call(
        functools.partial(body, **kw) if kw else body,
        out_shape=out,
        in_specs=[spec] * len(args),
        out_specs=[spec] * len(out) if isinstance(out, list) else spec,
        compiler_params=pltpu.CompilerParams(vmem_limit_bytes=GRANT),
        cost_estimate=pl.CostEstimate(flops=flops, bytes_accessed=moved, transcendentals=0),
        name=body.__name__,
    )(*args)


def per_device(array_volts, reference_volts, *, n_row):
    subs, _, ants, samples = array_volts.shape
    nref = reference_volts.shape[2]
    group = n_row // 2
    tiles = samples // group // LANES
    f32 = jnp.float32
    height = subs * 2 * tiles * ants
    message = call(
        pack_body,
        jax.ShapeDtypeStruct((n_row, height, LANES), jnp.bfloat16),
        array_volts,
        group=group,
    )
    volts = lax.all_to_all(message, "row", split_axis=0, concat_axis=0, tiled=True)
    crosses = call(
        cross_body,
        jax.ShapeDtypeStruct((1, (subs + 1) // 2 * ants, LANES), f32),
        array_volts,
        reference_volts,
        flops=10**8,
        moved=10**6,
    )
    bit = 1
    while bit < n_row:
        last = 2 * bit == n_row
        if last:
            volts, crosses = lax.optimization_barrier((volts, crosses))
        with jax.named_scope("last_hop" if last else "hop"):
            other = swap(crosses, bit, n_row)
        crosses = jnp.concatenate([crosses, other], 0)
        bit *= 2
    system = call(
        system_body,
        pltpu.VMEM((2, subs, nref, nref + ants), f32),
        array_volts,
        reference_volts,
        flops=10**9,
        moved=2 * 10**7,
    )
    solved = call(
        solve_body,
        pltpu.VMEM((subs, 2, nref, ants), f32),
        system,
        inner=(0,),
        flops=10**9,
        moved=2 * 10**7,
    )
    volts, solved = lax.optimization_barrier((volts, solved))
    half = pltpu.VMEM((group // 2, subs * 2 * ants, n_row * ants), f32)
    even, odd = call(
        product_body,
        [half, half],
        volts,
        inner=(0,),
        group=group,
        subs=subs,
        ants=ants,
    )
    sums = even + swap(odd, 1, n_row)
    parts = [sums[:1]] + [swap(sums[k : k + 1], 2 * k, n_row) for k in range(1, group // 2)]
    correction = call(
        correction_body,
        pltpu.VMEM((subs, 2, ants, n_row * ants), f32),
        crosses,
        solved,
        inner=(0, 1),
        flops=10**8,
        moved=2 * 10**6,
    )
    return call(
        finish_body,
        jax.ShapeDtypeStruct((subs, 2, ants, n_row * ants), f32),
        *parts,
        correction,
        inner=range(len(parts) + 1),
        samples=samples,
    )


def solution(mesh):
    n_row, n_col = mesh.shape["row"], mesh.shape["col"]

    def body(array_volts, reference_volts):
        samples = array_volts.shape[3]
        nref = reference_volts.shape[2]
        split = n_col == 1 and n_row > 1 and n_row & (n_row - 1) == 0 and samples % (n_row // 2 * LANES) == 0
        if split and 4 * nref == LANES:
            return per_device(array_volts, reference_volts, n_row=n_row)
        return per_device_any(array_volts, reference_volts)

    return jax.shard_map(
        body,
        mesh=mesh,
        in_specs=(P("chan", None, ("row", "col"), None), P("chan", None, None, "col")),
        out_specs=P("chan", None, "row", "col"),
        check_vma=False,
    )
```

```python
import functools

import jax
import jax.numpy as jnp
from jax import lax
from jax.experimental import pallas as pl
from jax.experimental.pallas import tpu as pltpu
from jax.sharding import PartitionSpec as P

LANES = 128
GRANT = 16 * 1024 * 1024
NT = (((1,), (1,)), ((), ()))
TN = (((0,), (0,)), ((), ()))
TT = (((0,), (1,)), ((), ()))
HIGHEST = lax.Precision.HIGHEST


def correlate(first_rows, second_rows):
    width_first = first_rows.shape[1]
    width_second = second_rows.shape[1]
    samples = first_rows.shape[2]
    stacked_first = first_rows.reshape(2 * width_first, samples)
    stacked_second = second_rows.reshape(2 * width_second, samples)
    product = jnp.einsum(
        "xn,yn->xy", stacked_first, stacked_second, preferred_element_type=jnp.float32
    )
    real_part = product[:width_first, :width_second] + product[width_first:, width_second:]
    imaginary_portion = product[width_first:, :width_second] - product[:width_first, width_second:]
    return jnp.stack([real_part, imaginary_portion]) / jnp.float32(samples)


def conj_swap(cross_block):
    return jnp.stack([cross_block[0].T, -cross_block[1].T])


def subtract(vis_tile, rows_cross, cross_cols, reference_covariance):
    real_cov = reference_covariance[0]
    imag_cov = reference_covariance[1]
    system = jnp.concatenate(
        [jnp.concatenate([real_cov, -imag_cov], 1), jnp.concatenate([imag_cov, real_cov], 1)], 0
    )
    lower_factor = jnp.linalg.cholesky(system)
    right_hand = jnp.concatenate([cross_cols[0], cross_cols[1]], 0)
    middle = lax.linalg.triangular_solve(lower_factor, right_hand, left_side=True, lower=True)
    solved = lax.linalg.triangular_solve(
        lower_factor, middle, left_side=True, lower=True, transpose_a=True
    )
    half_size = real_cov.shape[0]
    solved_real = solved[:half_size]
    solved_imag = solved[half_size:]
    corr_real = jnp.dot(rows_cross[0], solved_real, precision=HIGHEST) - jnp.dot(
        rows_cross[1], solved_imag, precision=HIGHEST
    )
    corr_imag = jnp.dot(rows_cross[0], solved_imag, precision=HIGHEST) + jnp.dot(
        rows_cross[1], solved_real, precision=HIGHEST
    )
    return vis_tile - jnp.stack([corr_real, corr_imag])


def per_device_any(array_volts, reference_volts):
    results = []
    for sub_index in range(array_volts.shape[0]):
        local_volts = array_volts[sub_index]
        ref_all = lax.all_gather(reference_volts[sub_index], "col", axis=2, tiled=True)
        reference_covariance = correlate(ref_all, ref_all)
        own_cross = correlate(ref_all, local_volts)
        cross_row_block = lax.all_gather(own_cross, "col", axis=2, tiled=True)
        cross_cols = lax.all_gather(own_cross, "row", axis=2, tiled=True)
        rows_cross = conj_swap(cross_row_block)
        row_volts = lax.all_gather(local_volts, "col", axis=1, tiled=True)
        joined = correlate(row_volts, lax.all_gather(local_volts, "row", axis=1, tiled=True))
        results.append(subtract(joined, rows_cross, cross_cols, reference_covariance))
    return jnp.stack(results)


def pack_body(volts_ref, message_ref, *, group):
    subs, _, ants, samples = volts_ref.shape
    members = message_ref.shape[0]
    share = samples // group
    tiles = share // LANES
    for s in range(subs):
        for p in range(2):
            for c in range(group):
                for t in range(tiles):
                    at = ((s * 2 + p) * tiles + t) * ants
                    start = c * share + t * LANES
                    block = volts_ref[s, p, :, start : start + LANES]
                    for m in range(c, members, group):
                        message_ref[m, at : at + ants, :] = block


def cross_body(volts_ref, reference_ref, message_ref):
    subs, _, ants, samples = volts_ref.shape
    crosses = []
    for s in range(subs):
        real, imag = volts_ref[s, 0], volts_ref[s, 1]
        ref_real, ref_imag = reference_ref[s, 0], reference_ref[s, 1]
        cross = lax.dot_general(
            real, jnp.concatenate([ref_real, -ref_imag], 0), NT, preferred_element_type=jnp.float32
        ) + lax.dot_general(
            imag, jnp.concatenate([ref_imag, ref_real], 0), NT, preferred_element_type=jnp.float32
        )
        crosses.append(cross / jnp.float32(samples))
    if subs % 2:
        crosses.append(jnp.zeros_like(crosses[0]))
    for pair in range(len(crosses) // 2):
        message_ref[0, pair * ants : (pair + 1) * ants, :] = jnp.concatenate(
            crosses[2 * pair : 2 * pair + 2], 1
        )


def system_body(volts_ref, reference_ref, system_ref):
    subs, _, ants, samples = volts_ref.shape
    nref = reference_ref.shape[2]
    dot = functools.partial(
        lax.dot_general, dimension_numbers=NT, preferred_element_type=jnp.float32
    )
    reals, imags = [], []
    for s in range(subs):
        real, imag = volts_ref[s, 0], volts_ref[s, 1]
        ref_real, ref_imag = reference_ref[s, 0], reference_ref[s, 1]
        first = jnp.concatenate([ref_real, real], 0)
        second = jnp.concatenate([ref_imag, imag], 0)
        reals.append((dot(ref_real, first) + dot(ref_imag, second)) / jnp.float32(samples))
        imags.append((dot(ref_imag, first) - dot(ref_real, second)) / jnp.float32(samples))
    re, im = eliminate(jnp.stack(reals), jnp.stack(imags), 0, nref // 2)
    system_ref[0], system_ref[1] = re, im


def solve_body(system_ref, solved_ref):
    nref = system_ref.shape[2]
    re, im = eliminate(system_ref[0], system_ref[1], nref // 2, nref)
    solved_ref[:, 0] = re[:, :, nref:]
    solved_ref[:, 1] = im[:, :, nref:]


def eliminate(re, im, start, stop):
    rows = lax.broadcasted_iota(jnp.int32, (1, re.shape[1], 1), 1)
    for i in range(start, stop):
        inverse = 1.0 / re[:, i : i + 1, i : i + 1]
        row_re, row_im = re[:, i : i + 1, :] * inverse, im[:, i : i + 1, :] * inverse
        col_re, col_im = re[:, :, i : i + 1], im[:, :, i : i + 1]
        here = rows == i
        re, im = (
            jnp.where(here, row_re, re - (col_re * row_re - col_im * row_im)),
            jnp.where(here, row_im, im - (col_re * row_im + col_im * row_re)),
        )
    return re, im


def joined(block):
    members, ants, lanes = block.shape
    return block.astype(jnp.float32).reshape(members * ants, lanes)


def product_body(message_ref, even_ref, odd_ref, *, group, subs, ants):
    members = message_ref.shape[0]
    tiles = message_ref.shape[1] // (ants * subs * 2)
    me = lax.axis_index("row")
    for s in range(subs):
        cols, own = [], []
        for p in range(2):
            for t in range(tiles):
                at = ((s * 2 + p) * tiles + t) * ants
                cols.append(joined(message_ref[:, at : at + ants, :]).astype(jnp.bfloat16))
                own.append(
                    jnp.concatenate(
                        [
                            message_ref[me ^ j, at : at + ants, :].astype(jnp.float32)
                            for j in range(group)
                        ],
                        0,
                    )
                )
        right = jnp.concatenate(cols, 1)
        upper = jnp.concatenate(own, 1)
        lower = jnp.concatenate(own[tiles:] + [-x for x in own[:tiles]], 1)
        left = jnp.concatenate([upper, lower], 0).astype(jnp.bfloat16)
        out = lax.dot_general(left, right, NT, preferred_element_type=jnp.float32)
        for p in range(2):
            at = (s * 2 + p) * ants
            for j in range(group):
                row = (p * group + j) * ants
                ref = odd_ref if j % 2 else even_ref
                ref[j // 2, at : at + ants, :] = out[row : row + ants]


def correction_body(cross_ref, solved_ref, correction_ref):
    subs, _, nref, ants = solved_ref.shape
    me = lax.axis_index("row")
    for pair in range((subs + 1) // 2):
        members = range(2 * pair, min(2 * pair + 2, subs))
        cross = jnp.concatenate(
            [
                cross_ref[me ^ m, pair * ants : (pair + 1) * ants, :]
                for m in range(cross_ref.shape[0])
            ],
            0,
        )
        columns = []
        for s in members:
            re, im = solved_ref[s, 0], solved_ref[s, 1]
            none = jnp.zeros((2 * nref, ants), jnp.float32)
            for stack in ([re, -im], [-im, -re]):
                columns.append(
                    jnp.concatenate(stack + [none] if s % 2 == 0 else [none] + stack, 0)
                )
        out = lax.dot_general(
            jnp.concatenate(columns, 1),
            cross,
            TT,
            precision=HIGHEST,
            preferred_element_type=jnp.float32,
        )
        for k, s in enumerate(members):
            for p in range(2):
                at = (2 * k + p) * ants
                correction_ref[s, p] = out[at : at + ants]


def finish_body(kept_ref, *refs, samples):
    *others, correction_ref, cleaned_ref = refs
    subs, _, ants, _ = cleaned_ref.shape
    total = kept_ref[0]
    for ref in others:
        total = total + ref[0]
    total = total / jnp.float32(samples)
    for s in range(subs):
        for p in range(2):
            at = (s * 2 + p) * ants
            cleaned_ref[s, p] = total[at : at + ants] - correction_ref[s, p]


def swap(x, bit, n_row):
    return lax.ppermute(x, "row", [(i, i ^ bit) for i in range(n_row)])


def call(body, out, *args, inner=(), flops=0, moved=0, **kw):
    spec = pl.BlockSpec(memory_space=pltpu.VMEM)
    args = [
        pltpu.with_memory_space_constraint(x, pltpu.VMEM) if i in inner else x
        for i, x in enumerate(args)
    ]
    return pl.pallas_call(
        functools.partial(body, **kw) if kw else body,
        out_shape=out,
        in_specs=[spec] * len(args),
        out_specs=[spec] * len(out) if isinstance(out, list) else spec,
        compiler_params=pltpu.CompilerParams(vmem_limit_bytes=GRANT),
        cost_estimate=pl.CostEstimate(flops=flops, bytes_accessed=moved, transcendentals=0),
        name=body.__name__,
    )(*args)


def per_device(array_volts, reference_volts, *, n_row):
    subs, _, ants, samples = array_volts.shape
    nref = reference_volts.shape[2]
    group = n_row // 2
    tiles = samples // group // LANES
    f32 = jnp.float32
    height = subs * 2 * tiles * ants
    message = call(
        pack_body,
        jax.ShapeDtypeStruct((n_row, height, LANES), jnp.bfloat16),
        array_volts,
        group=group,
    )
    volts = lax.all_to_all(message, "row", split_axis=0, concat_axis=0, tiled=True)
    crosses = call(
        cross_body,
        jax.ShapeDtypeStruct((1, (subs + 1) // 2 * ants, LANES), f32),
        array_volts,
        reference_volts,
        flops=10**8,
        moved=10**6,
    )
    bit = 1
    while bit < n_row:
        last = 2 * bit == n_row
        if last:
            volts, crosses = lax.optimization_barrier((volts, crosses))
        with jax.named_scope("last_hop" if last else "hop"):
            other = swap(crosses, bit, n_row)
        crosses = jnp.concatenate([crosses, other], 0)
        bit *= 2
    system = call(
        system_body,
        pltpu.VMEM((2, subs, nref, nref + ants), f32),
        array_volts,
        reference_volts,
        flops=10**9,
        moved=2 * 10**7,
    )
    solved = call(
        solve_body,
        pltpu.VMEM((subs, 2, nref, ants), f32),
        system,
        inner=(0,),
        flops=10**9,
        moved=2 * 10**7,
    )
    volts, solved = lax.optimization_barrier((volts, solved))
    half = pltpu.VMEM((group // 2, subs * 2 * ants, n_row * ants), f32)
    even, odd = call(
        product_body,
        [half, half],
        volts,
        inner=(0,),
        group=group,
        subs=subs,
        ants=ants,
    )
    sums = even + swap(odd, 1, n_row)
    parts = [swap(sums[k : k + 1], 2 * k, n_row) for k in range(group // 2 - 1, 0, -1)]
    parts.append(sums[:1])
    correction = call(
        correction_body,
        pltpu.VMEM((subs, 2, ants, n_row * ants), f32),
        crosses,
        solved,
        inner=(0, 1),
        flops=10**8,
        moved=2 * 10**6,
    )
    return call(
        finish_body,
        jax.ShapeDtypeStruct((subs, 2, ants, n_row * ants), f32),
        *parts,
        correction,
        inner=range(len(parts) + 1),
        samples=samples,
    )


def solution(mesh):
    n_row, n_col = mesh.shape["row"], mesh.shape["col"]

    def body(array_volts, reference_volts):
        samples = array_volts.shape[3]
        nref = reference_volts.shape[2]
        split = n_col == 1 and n_row > 1 and n_row & (n_row - 1) == 0 and samples % (n_row // 2 * LANES) == 0
        if split and 4 * nref == LANES:
            return per_device(array_volts, reference_volts, n_row=n_row)
        return per_device_any(array_volts, reference_volts)

    return jax.shard_map(
        body,
        mesh=mesh,
        in_specs=(P("chan", None, ("row", "col"), None), P("chan", None, None, "col")),
        out_specs=P("chan", None, "row", "col"),
        check_vma=False,
    )
```

```python
import functools

import jax
import jax.numpy as jnp
from jax import lax
from jax.experimental import pallas as pl
from jax.experimental.pallas import tpu as pltpu
from jax.sharding import PartitionSpec as P

LANES = 128
GRANT = 16 * 1024 * 1024
NT = (((1,), (1,)), ((), ()))
TN = (((0,), (0,)), ((), ()))
TT = (((0,), (1,)), ((), ()))
HIGHEST = lax.Precision.HIGHEST


def correlate(first_rows, second_rows):
    width_first = first_rows.shape[1]
    width_second = second_rows.shape[1]
    samples = first_rows.shape[2]
    stacked_first = first_rows.reshape(2 * width_first, samples)
    stacked_second = second_rows.reshape(2 * width_second, samples)
    product = jnp.einsum(
        "xn,yn->xy", stacked_first, stacked_second, preferred_element_type=jnp.float32
    )
    real_part = product[:width_first, :width_second] + product[width_first:, width_second:]
    imaginary_portion = product[width_first:, :width_second] - product[:width_first, width_second:]
    return jnp.stack([real_part, imaginary_portion]) / jnp.float32(samples)


def conj_swap(cross_block):
    return jnp.stack([cross_block[0].T, -cross_block[1].T])


def subtract(vis_tile, rows_cross, cross_cols, reference_covariance):
    real_cov = reference_covariance[0]
    imag_cov = reference_covariance[1]
    system = jnp.concatenate(
        [jnp.concatenate([real_cov, -imag_cov], 1), jnp.concatenate([imag_cov, real_cov], 1)], 0
    )
    lower_factor = jnp.linalg.cholesky(system)
    right_hand = jnp.concatenate([cross_cols[0], cross_cols[1]], 0)
    middle = lax.linalg.triangular_solve(lower_factor, right_hand, left_side=True, lower=True)
    solved = lax.linalg.triangular_solve(
        lower_factor, middle, left_side=True, lower=True, transpose_a=True
    )
    half_size = real_cov.shape[0]
    solved_real = solved[:half_size]
    solved_imag = solved[half_size:]
    corr_real = jnp.dot(rows_cross[0], solved_real, precision=HIGHEST) - jnp.dot(
        rows_cross[1], solved_imag, precision=HIGHEST
    )
    corr_imag = jnp.dot(rows_cross[0], solved_imag, precision=HIGHEST) + jnp.dot(
        rows_cross[1], solved_real, precision=HIGHEST
    )
    return vis_tile - jnp.stack([corr_real, corr_imag])


def per_device_any(array_volts, reference_volts):
    results = []
    for sub_index in range(array_volts.shape[0]):
        local_volts = array_volts[sub_index]
        ref_all = lax.all_gather(reference_volts[sub_index], "col", axis=2, tiled=True)
        reference_covariance = correlate(ref_all, ref_all)
        own_cross = correlate(ref_all, local_volts)
        cross_row_block = lax.all_gather(own_cross, "col", axis=2, tiled=True)
        cross_cols = lax.all_gather(own_cross, "row", axis=2, tiled=True)
        rows_cross = conj_swap(cross_row_block)
        row_volts = lax.all_gather(local_volts, "col", axis=1, tiled=True)
        joined = correlate(row_volts, lax.all_gather(local_volts, "row", axis=1, tiled=True))
        results.append(subtract(joined, rows_cross, cross_cols, reference_covariance))
    return jnp.stack(results)


def pack_body(volts_ref, message_ref, *, group):
    subs, _, ants, samples = volts_ref.shape
    members = message_ref.shape[0]
    share = samples // group
    tiles = share // LANES
    for s in range(subs):
        for p in range(2):
            for c in range(group):
                for t in range(tiles):
                    at = ((s * 2 + p) * tiles + t) * ants
                    start = c * share + t * LANES
                    block = volts_ref[s, p, :, start : start + LANES]
                    for m in range(c, members, group):
                        message_ref[m, at : at + ants, :] = block


def cross_body(volts_ref, reference_ref, message_ref):
    subs, _, ants, samples = volts_ref.shape
    crosses = []
    for s in range(subs):
        real, imag = volts_ref[s, 0], volts_ref[s, 1]
        ref_real, ref_imag = reference_ref[s, 0], reference_ref[s, 1]
        cross = lax.dot_general(
            real, jnp.concatenate([ref_real, -ref_imag], 0), NT, preferred_element_type=jnp.float32
        ) + lax.dot_general(
            imag, jnp.concatenate([ref_imag, ref_real], 0), NT, preferred_element_type=jnp.float32
        )
        crosses.append(cross / jnp.float32(samples))
    if subs % 2:
        crosses.append(jnp.zeros_like(crosses[0]))
    for pair in range(len(crosses) // 2):
        message_ref[0, pair * ants : (pair + 1) * ants, :] = jnp.concatenate(
            crosses[2 * pair : 2 * pair + 2], 1
        )


def system_body(volts_ref, reference_ref, system_ref):
    subs, _, ants, samples = volts_ref.shape
    nref = reference_ref.shape[2]
    dot = functools.partial(
        lax.dot_general, dimension_numbers=NT, preferred_element_type=jnp.float32
    )
    reals, imags = [], []
    for s in range(subs):
        real, imag = volts_ref[s, 0], volts_ref[s, 1]
        ref_real, ref_imag = reference_ref[s, 0], reference_ref[s, 1]
        first = jnp.concatenate([ref_real, real], 0)
        second = jnp.concatenate([ref_imag, imag], 0)
        reals.append((dot(ref_real, first) + dot(ref_imag, second)) / jnp.float32(samples))
        imags.append((dot(ref_imag, first) - dot(ref_real, second)) / jnp.float32(samples))
    re, im = eliminate(jnp.stack(reals), jnp.stack(imags), 0, nref // 2)
    system_ref[0], system_ref[1] = re, im


def solve_body(system_ref, solved_ref):
    nref = system_ref.shape[2]
    re, im = eliminate(system_ref[0], system_ref[1], nref // 2, nref)
    solved_ref[:, 0] = re[:, :, nref:]
    solved_ref[:, 1] = im[:, :, nref:]


def eliminate(re, im, start, stop):
    rows = lax.broadcasted_iota(jnp.int32, (1, re.shape[1], 1), 1)
    for i in range(start, stop):
        inverse = 1.0 / re[:, i : i + 1, i : i + 1]
        row_re, row_im = re[:, i : i + 1, :] * inverse, im[:, i : i + 1, :] * inverse
        col_re, col_im = re[:, :, i : i + 1], im[:, :, i : i + 1]
        here = rows == i
        re, im = (
            jnp.where(here, row_re, re - (col_re * row_re - col_im * row_im)),
            jnp.where(here, row_im, im - (col_re * row_im + col_im * row_re)),
        )
    return re, im


def joined(block):
    members, ants, lanes = block.shape
    return block.astype(jnp.float32).reshape(members * ants, lanes)


def product_body(message_ref, even_ref, odd_ref, *, group, subs, ants):
    members = message_ref.shape[0]
    tiles = message_ref.shape[1] // (ants * subs * 2)
    me = lax.axis_index("row")
    for s in range(subs):
        cols, own = [], []
        for p in range(2):
            for t in range(tiles):
                at = ((s * 2 + p) * tiles + t) * ants
                cols.append(joined(message_ref[:, at : at + ants, :]).astype(jnp.bfloat16))
                own.append(
                    jnp.concatenate(
                        [
                            message_ref[me ^ j, at : at + ants, :].astype(jnp.float32)
                            for j in range(group)
                        ],
                        0,
                    )
                )
        right = jnp.concatenate(cols, 1)
        upper = jnp.concatenate(own, 1)
        lower = jnp.concatenate(own[tiles:] + [-x for x in own[:tiles]], 1)
        left = jnp.concatenate([upper, lower], 0).astype(jnp.bfloat16)
        out = lax.dot_general(left, right, NT, preferred_element_type=jnp.float32)
        for p in range(2):
            at = (s * 2 + p) * ants
            for j in range(group):
                row = (p * group + j) * ants
                ref = odd_ref if j % 2 else even_ref
                ref[j // 2, at : at + ants, :] = out[row : row + ants]


def correction_body(cross_ref, solved_ref, correction_ref):
    subs, _, nref, ants = solved_ref.shape
    count = correction_ref.shape[3] // ants
    whole = subs // 2 * ants
    me = lax.axis_index("row")
    none = jnp.zeros((2 * nref, ants), jnp.float32)

    def product(columns, cross):
        return lax.dot_general(
            jnp.concatenate(columns, 1),
            cross,
            TT,
            precision=HIGHEST,
            preferred_element_type=jnp.float32,
        )

    def stacks(s):
        re, im = solved_ref[s, 0], solved_ref[s, 1]
        return [re, -im], [-im, -re]

    for first in range(0, subs - 1, 2):
        cross = jnp.concatenate(
            [
                cross_ref[
                    (me ^ m) // 2,
                    pl.ds(pl.multiple_of((me ^ m) % 2 * whole + first // 2 * ants, 8), ants),
                    :,
                ]
                for m in range(count)
            ],
            0,
        )
        columns = [jnp.concatenate(stack + [none], 0) for stack in stacks(first)]
        columns += [jnp.concatenate([none] + stack, 0) for stack in stacks(first + 1)]
        out = product(columns, cross)
        for k in range(2):
            for p in range(2):
                at = (2 * k + p) * ants
                correction_ref[first + k, p] = out[at : at + ants]
    if subs % 2:
        cross = jnp.concatenate(
            [cross_ref[(me ^ m) // 2, 2 * whole : 2 * whole + ants, :] for m in range(count)], 0
        )
        columns = [jnp.concatenate(stack + [none], 0) for stack in stacks(subs - 1)]
        columns += [jnp.concatenate([none] + stack, 0) for stack in stacks(subs - 1)]
        out = product(columns, cross)
        owner = lax.broadcasted_iota(jnp.int32, (ants, count * ants), 1) // ants
        lower = (owner ^ me) % 2 == 0
        for p in range(2):
            low, high = out[p * ants : (p + 1) * ants], out[(2 + p) * ants : (3 + p) * ants]
            correction_ref[subs - 1, p] = jnp.where(lower, low, high)


def finish_body(kept_ref, *refs, samples):
    *others, correction_ref, cleaned_ref = refs
    subs, _, ants, _ = cleaned_ref.shape
    total = kept_ref[0]
    for ref in others:
        total = total + ref[0]
    total = total / jnp.float32(samples)
    for s in range(subs):
        for p in range(2):
            at = (s * 2 + p) * ants
            cleaned_ref[s, p] = total[at : at + ants] - correction_ref[s, p]


def chip(mine, partner, subs, ants):
    whole = subs // 2 * ants
    parts = [mine[:, :whole], partner[:, :whole]]
    if subs % 2:
        half = mine.shape[2] // 2
        parts.append(jnp.concatenate([mine[:, whole:, :half], partner[:, whole:, :half]], 2))
    return jnp.concatenate(parts, 1)


def swap(x, bit, n_row):
    return lax.ppermute(x, "row", [(i, i ^ bit) for i in range(n_row)])


def call(body, out, *args, inner=(), flops=0, moved=0, **kw):
    spec = pl.BlockSpec(memory_space=pltpu.VMEM)
    args = [
        pltpu.with_memory_space_constraint(x, pltpu.VMEM) if i in inner else x
        for i, x in enumerate(args)
    ]
    return pl.pallas_call(
        functools.partial(body, **kw) if kw else body,
        out_shape=out,
        in_specs=[spec] * len(args),
        out_specs=[spec] * len(out) if isinstance(out, list) else spec,
        compiler_params=pltpu.CompilerParams(vmem_limit_bytes=GRANT),
        cost_estimate=pl.CostEstimate(flops=flops, bytes_accessed=moved, transcendentals=0),
        name=body.__name__,
    )(*args)


def per_device(array_volts, reference_volts, *, n_row):
    subs, _, ants, samples = array_volts.shape
    nref = reference_volts.shape[2]
    group = n_row // 2
    tiles = samples // group // LANES
    f32 = jnp.float32
    height = subs * 2 * tiles * ants
    message = call(
        pack_body,
        jax.ShapeDtypeStruct((n_row, height, LANES), jnp.bfloat16),
        array_volts,
        group=group,
    )
    volts = lax.all_to_all(message, "row", split_axis=0, concat_axis=0, tiled=True)
    crosses = call(
        cross_body,
        jax.ShapeDtypeStruct((1, (subs + 1) // 2 * ants, LANES), f32),
        array_volts,
        reference_volts,
        flops=10**8,
        moved=10**6,
    )
    bit = 1
    while bit < n_row:
        last = 2 * bit == n_row
        if last:
            volts, crosses = lax.optimization_barrier((volts, crosses))
        with jax.named_scope("last_hop" if last else "hop"):
            other = swap(crosses, bit, n_row)
        crosses = jnp.concatenate([crosses, other], 0) if bit > 1 else chip(crosses, other, subs, ants)
        bit *= 2
    system = call(
        system_body,
        pltpu.VMEM((2, subs, nref, nref + ants), f32),
        array_volts,
        reference_volts,
        flops=10**9,
        moved=2 * 10**7,
    )
    solved = call(
        solve_body,
        pltpu.VMEM((subs, 2, nref, ants), f32),
        system,
        inner=(0,),
        flops=10**9,
        moved=2 * 10**7,
    )
    volts, solved = lax.optimization_barrier((volts, solved))
    half = pltpu.VMEM((group // 2, subs * 2 * ants, n_row * ants), f32)
    even, odd = call(
        product_body,
        [half, half],
        volts,
        inner=(0,),
        group=group,
        subs=subs,
        ants=ants,
    )
    sums = even + swap(odd, 1, n_row)
    parts = [swap(sums[k : k + 1], 2 * k, n_row) for k in range(group // 2 - 1, 0, -1)]
    parts.append(sums[:1])
    correction = call(
        correction_body,
        pltpu.VMEM((subs, 2, ants, n_row * ants), f32),
        crosses,
        solved,
        inner=(0, 1),
        flops=10**8,
        moved=2 * 10**6,
    )
    return call(
        finish_body,
        jax.ShapeDtypeStruct((subs, 2, ants, n_row * ants), f32),
        *parts,
        correction,
        inner=range(len(parts) + 1),
        samples=samples,
    )


def solution(mesh):
    n_row, n_col = mesh.shape["row"], mesh.shape["col"]

    def body(array_volts, reference_volts):
        samples = array_volts.shape[3]
        nref = reference_volts.shape[2]
        split = n_col == 1 and n_row > 1 and n_row & (n_row - 1) == 0 and samples % (n_row // 2 * LANES) == 0
        if split and 4 * nref == LANES:
            return per_device(array_volts, reference_volts, n_row=n_row)
        return per_device_any(array_volts, reference_volts)

    return jax.shard_map(
        body,
        mesh=mesh,
        in_specs=(P("chan", None, ("row", "col"), None), P("chan", None, None, "col")),
        out_specs=P("chan", None, "row", "col"),
        check_vma=False,
    )
```

```python
import functools

import jax
import jax.numpy as jnp
from jax import lax
from jax.experimental import pallas as pl
from jax.experimental.pallas import tpu as pltpu
from jax.sharding import PartitionSpec as P

LANES = 128
GRANT = 16 * 1024 * 1024
NT = (((1,), (1,)), ((), ()))
TN = (((0,), (0,)), ((), ()))
TT = (((0,), (1,)), ((), ()))
HIGHEST = lax.Precision.HIGHEST


def correlate(first_rows, second_rows):
    width_first = first_rows.shape[1]
    width_second = second_rows.shape[1]
    samples = first_rows.shape[2]
    stacked_first = first_rows.reshape(2 * width_first, samples)
    stacked_second = second_rows.reshape(2 * width_second, samples)
    product = jnp.einsum(
        "xn,yn->xy", stacked_first, stacked_second, preferred_element_type=jnp.float32
    )
    real_part = product[:width_first, :width_second] + product[width_first:, width_second:]
    imaginary_portion = product[width_first:, :width_second] - product[:width_first, width_second:]
    return jnp.stack([real_part, imaginary_portion]) / jnp.float32(samples)


def conj_swap(cross_block):
    return jnp.stack([cross_block[0].T, -cross_block[1].T])


def subtract(vis_tile, rows_cross, cross_cols, reference_covariance):
    real_cov = reference_covariance[0]
    imag_cov = reference_covariance[1]
    system = jnp.concatenate(
        [jnp.concatenate([real_cov, -imag_cov], 1), jnp.concatenate([imag_cov, real_cov], 1)], 0
    )
    lower_factor = jnp.linalg.cholesky(system)
    right_hand = jnp.concatenate([cross_cols[0], cross_cols[1]], 0)
    middle = lax.linalg.triangular_solve(lower_factor, right_hand, left_side=True, lower=True)
    solved = lax.linalg.triangular_solve(
        lower_factor, middle, left_side=True, lower=True, transpose_a=True
    )
    half_size = real_cov.shape[0]
    solved_real = solved[:half_size]
    solved_imag = solved[half_size:]
    corr_real = jnp.dot(rows_cross[0], solved_real, precision=HIGHEST) - jnp.dot(
        rows_cross[1], solved_imag, precision=HIGHEST
    )
    corr_imag = jnp.dot(rows_cross[0], solved_imag, precision=HIGHEST) + jnp.dot(
        rows_cross[1], solved_real, precision=HIGHEST
    )
    return vis_tile - jnp.stack([corr_real, corr_imag])


def per_device_any(array_volts, reference_volts):
    results = []
    for sub_index in range(array_volts.shape[0]):
        local_volts = array_volts[sub_index]
        ref_all = lax.all_gather(reference_volts[sub_index], "col", axis=2, tiled=True)
        reference_covariance = correlate(ref_all, ref_all)
        own_cross = correlate(ref_all, local_volts)
        cross_row_block = lax.all_gather(own_cross, "col", axis=2, tiled=True)
        cross_cols = lax.all_gather(own_cross, "row", axis=2, tiled=True)
        rows_cross = conj_swap(cross_row_block)
        row_volts = lax.all_gather(local_volts, "col", axis=1, tiled=True)
        joined = correlate(row_volts, lax.all_gather(local_volts, "row", axis=1, tiled=True))
        results.append(subtract(joined, rows_cross, cross_cols, reference_covariance))
    return jnp.stack(results)


def pack_body(volts_ref, message_ref, *, group):
    subs, _, ants, samples = volts_ref.shape
    members = message_ref.shape[0]
    share = samples // group
    tiles = share // LANES
    for s in range(subs):
        for p in range(2):
            for c in range(group):
                for t in range(tiles):
                    at = ((s * 2 + p) * tiles + t) * ants
                    start = c * share + t * LANES
                    block = volts_ref[s, p, :, start : start + LANES]
                    for m in range(c, members, group):
                        message_ref[m, at : at + ants, :] = block


def cross_body(volts_ref, reference_ref, message_ref):
    subs, _, ants, samples = volts_ref.shape
    crosses = []
    for s in range(subs):
        real, imag = volts_ref[s, 0], volts_ref[s, 1]
        ref_real, ref_imag = reference_ref[s, 0], reference_ref[s, 1]
        cross = lax.dot_general(
            real, jnp.concatenate([ref_real, -ref_imag], 0), NT, preferred_element_type=jnp.float32
        ) + lax.dot_general(
            imag, jnp.concatenate([ref_imag, ref_real], 0), NT, preferred_element_type=jnp.float32
        )
        crosses.append(cross / jnp.float32(samples))
    if subs % 2:
        crosses.append(jnp.zeros_like(crosses[0]))
    for pair in range(len(crosses) // 2):
        message_ref[0, pair * ants : (pair + 1) * ants, :] = jnp.concatenate(
            crosses[2 * pair : 2 * pair + 2], 1
        )


def system_body(volts_ref, reference_ref, system_ref):
    subs, _, ants, samples = volts_ref.shape
    nref = reference_ref.shape[2]
    dot = functools.partial(
        lax.dot_general, dimension_numbers=NT, preferred_element_type=jnp.float32
    )
    reals, imags = [], []
    for s in range(subs):
        real, imag = volts_ref[s, 0], volts_ref[s, 1]
        ref_real, ref_imag = reference_ref[s, 0], reference_ref[s, 1]
        first = jnp.concatenate([ref_real, real], 0)
        second = jnp.concatenate([ref_imag, imag], 0)
        reals.append((dot(ref_real, first) + dot(ref_imag, second)) / jnp.float32(samples))
        imags.append((dot(ref_imag, first) - dot(ref_real, second)) / jnp.float32(samples))
    re, im = eliminate(jnp.stack(reals), jnp.stack(imags), 0, 3 * nref // 8)
    system_ref[0], system_ref[1] = re, im


def solve_body(system_ref, solved_ref):
    nref = system_ref.shape[2]
    re, im = eliminate(system_ref[0], system_ref[1], 3 * nref // 8, nref)
    solved_ref[:, 0] = re[:, :, nref:]
    solved_ref[:, 1] = im[:, :, nref:]


def eliminate(re, im, start, stop):
    rows = lax.broadcasted_iota(jnp.int32, (1, re.shape[1], 1), 1)
    for i in range(start, stop):
        inverse = 1.0 / re[:, i : i + 1, i : i + 1]
        row_re, row_im = re[:, i : i + 1, :] * inverse, im[:, i : i + 1, :] * inverse
        col_re, col_im = re[:, :, i : i + 1], im[:, :, i : i + 1]
        here = rows == i
        re, im = (
            jnp.where(here, row_re, re - (col_re * row_re - col_im * row_im)),
            jnp.where(here, row_im, im - (col_re * row_im + col_im * row_re)),
        )
    return re, im


def joined(block):
    members, ants, lanes = block.shape
    return block.astype(jnp.float32).reshape(members * ants, lanes)


def product_body(message_ref, even_ref, odd_ref, *, group, subs, ants):
    members = message_ref.shape[0]
    tiles = message_ref.shape[1] // (ants * subs * 2)
    me = lax.axis_index("row")
    for s in range(subs):
        cols, own = [], []
        for p in range(2):
            for t in range(tiles):
                at = ((s * 2 + p) * tiles + t) * ants
                cols.append(joined(message_ref[:, at : at + ants, :]).astype(jnp.bfloat16))
                own.append(
                    jnp.concatenate(
                        [
                            message_ref[me ^ j, at : at + ants, :].astype(jnp.float32)
                            for j in range(group)
                        ],
                        0,
                    )
                )
        right = jnp.concatenate(cols, 1)
        upper = jnp.concatenate(own, 1)
        lower = jnp.concatenate(own[tiles:] + [-x for x in own[:tiles]], 1)
        left = jnp.concatenate([upper, lower], 0).astype(jnp.bfloat16)
        out = lax.dot_general(left, right, NT, preferred_element_type=jnp.float32)
        for p in range(2):
            at = (s * 2 + p) * ants
            for j in range(group):
                row = (p * group + j) * ants
                ref = odd_ref if j % 2 else even_ref
                ref[j // 2, at : at + ants, :] = out[row : row + ants]


def correction_body(cross_ref, solved_ref, correction_ref):
    subs, _, nref, ants = solved_ref.shape
    count = correction_ref.shape[3] // ants
    whole = subs // 2 * ants
    me = lax.axis_index("row")
    none = jnp.zeros((2 * nref, ants), jnp.float32)

    def product(columns, cross):
        return lax.dot_general(
            jnp.concatenate(columns, 1),
            cross,
            TT,
            precision=HIGHEST,
            preferred_element_type=jnp.float32,
        )

    def stacks(s):
        re, im = solved_ref[s, 0], solved_ref[s, 1]
        return [re, -im], [-im, -re]

    for first in range(0, subs - 1, 2):
        cross = jnp.concatenate(
            [
                cross_ref[
                    (me ^ m) // 2,
                    pl.ds(pl.multiple_of((me ^ m) % 2 * whole + first // 2 * ants, 8), ants),
                    :,
                ]
                for m in range(count)
            ],
            0,
        )
        columns = [jnp.concatenate(stack + [none], 0) for stack in stacks(first)]
        columns += [jnp.concatenate([none] + stack, 0) for stack in stacks(first + 1)]
        out = product(columns, cross)
        for k in range(2):
            for p in range(2):
                at = (2 * k + p) * ants
                correction_ref[first + k, p] = out[at : at + ants]
    if subs % 2:
        cross = jnp.concatenate(
            [cross_ref[(me ^ m) // 2, 2 * whole : 2 * whole + ants, :] for m in range(count)], 0
        )
        columns = [jnp.concatenate(stack + [none], 0) for stack in stacks(subs - 1)]
        columns += [jnp.concatenate([none] + stack, 0) for stack in stacks(subs - 1)]
        out = product(columns, cross)
        owner = lax.broadcasted_iota(jnp.int32, (ants, count * ants), 1) // ants
        lower = (owner ^ me) % 2 == 0
        for p in range(2):
            low, high = out[p * ants : (p + 1) * ants], out[(2 + p) * ants : (3 + p) * ants]
            correction_ref[subs - 1, p] = jnp.where(lower, low, high)


def finish_body(kept_ref, *refs, samples):
    *others, correction_ref, cleaned_ref = refs
    subs, _, ants, _ = cleaned_ref.shape
    total = kept_ref[0]
    for ref in others:
        total = total + ref[0]
    total = total / jnp.float32(samples)
    for s in range(subs):
        for p in range(2):
            at = (s * 2 + p) * ants
            cleaned_ref[s, p] = total[at : at + ants] - correction_ref[s, p]


def chip(mine, partner, subs, ants):
    whole = subs // 2 * ants
    parts = [mine[:, :whole], partner[:, :whole]]
    if subs % 2:
        half = mine.shape[2] // 2
        parts.append(jnp.concatenate([mine[:, whole:, :half], partner[:, whole:, :half]], 2))
    return jnp.concatenate(parts, 1)


def swap(x, bit, n_row):
    return lax.ppermute(x, "row", [(i, i ^ bit) for i in range(n_row)])


def call(body, out, *args, inner=(), flops=0, moved=0, **kw):
    spec = pl.BlockSpec(memory_space=pltpu.VMEM)
    args = [
        pltpu.with_memory_space_constraint(x, pltpu.VMEM) if i in inner else x
        for i, x in enumerate(args)
    ]
    return pl.pallas_call(
        functools.partial(body, **kw) if kw else body,
        out_shape=out,
        in_specs=[spec] * len(args),
        out_specs=[spec] * len(out) if isinstance(out, list) else spec,
        compiler_params=pltpu.CompilerParams(vmem_limit_bytes=GRANT),
        cost_estimate=pl.CostEstimate(flops=flops, bytes_accessed=moved, transcendentals=0),
        name=body.__name__,
    )(*args)


def per_device(array_volts, reference_volts, *, n_row):
    subs, _, ants, samples = array_volts.shape
    nref = reference_volts.shape[2]
    group = n_row // 2
    tiles = samples // group // LANES
    f32 = jnp.float32
    height = subs * 2 * tiles * ants
    message = call(
        pack_body,
        jax.ShapeDtypeStruct((n_row, height, LANES), jnp.bfloat16),
        array_volts,
        group=group,
    )
    volts = lax.all_to_all(message, "row", split_axis=0, concat_axis=0, tiled=True)
    crosses = call(
        cross_body,
        jax.ShapeDtypeStruct((1, (subs + 1) // 2 * ants, LANES), f32),
        array_volts,
        reference_volts,
        flops=10**8,
        moved=10**6,
    )
    bit = 1
    while bit < n_row:
        last = 2 * bit == n_row
        if last:
            volts, crosses = lax.optimization_barrier((volts, crosses))
        with jax.named_scope("last_hop" if last else "hop"):
            other = swap(crosses, bit, n_row)
        crosses = jnp.concatenate([crosses, other], 0) if bit > 1 else chip(crosses, other, subs, ants)
        bit *= 2
    system = call(
        system_body,
        pltpu.VMEM((2, subs, nref, nref + ants), f32),
        array_volts,
        reference_volts,
        flops=10**9,
        moved=2 * 10**7,
    )
    solved = call(
        solve_body,
        pltpu.VMEM((subs, 2, nref, ants), f32),
        system,
        inner=(0,),
        flops=10**9,
        moved=2 * 10**7,
    )
    volts, solved = lax.optimization_barrier((volts, solved))
    half = pltpu.VMEM((group // 2, subs * 2 * ants, n_row * ants), f32)
    even, odd = call(
        product_body,
        [half, half],
        volts,
        inner=(0,),
        group=group,
        subs=subs,
        ants=ants,
    )
    sums = even + swap(odd, 1, n_row)
    parts = [swap(sums[k : k + 1], 2 * k, n_row) for k in range(group // 2 - 1, 0, -1)]
    parts.append(sums[:1])
    correction = call(
        correction_body,
        pltpu.VMEM((subs, 2, ants, n_row * ants), f32),
        crosses,
        solved,
        inner=(0, 1),
        flops=10**8,
        moved=2 * 10**6,
    )
    return call(
        finish_body,
        jax.ShapeDtypeStruct((subs, 2, ants, n_row * ants), f32),
        *parts,
        correction,
        inner=range(len(parts) + 1),
        samples=samples,
    )


def solution(mesh):
    n_row, n_col = mesh.shape["row"], mesh.shape["col"]

    def body(array_volts, reference_volts):
        samples = array_volts.shape[3]
        nref = reference_volts.shape[2]
        split = n_col == 1 and n_row > 1 and n_row & (n_row - 1) == 0 and samples % (n_row // 2 * LANES) == 0
        if split and 4 * nref == LANES:
            return per_device(array_volts, reference_volts, n_row=n_row)
        return per_device_any(array_volts, reference_volts)

    return jax.shard_map(
        body,
        mesh=mesh,
        in_specs=(P("chan", None, ("row", "col"), None), P("chan", None, None, "col")),
        out_specs=P("chan", None, "row", "col"),
        check_vma=False,
    )
```
